32 devices in a mesh: grp: 4 (over z), term: 8 (over y, x, core).
Axes of the slice: x: 2, y: 2, z: 4, core: 2. Of those that a mesh axis runs over, the one named last changes fastest.
Arguments:
- hidden_states: bfloat16 [16384, 768], P(('grp', 'term')), may hold values from -8 to 8
- lengths: int32 [128], P(('grp', 'term')), may hold values from 32 to 128, as said below
- block_list: int32 [128, 96], P(('grp', 'term')), may hold values from 0 to 128, as said below
- cluster_ids: int32 [128], P(('grp', 'term')), may hold values from 0 to 16383, as said below
- attn_weight: bfloat16 [768, 2304], replicated, may hold values from -4 to 4
- out_weight: bfloat16 [768, 768], replicated, may hold values from -0.21875 to 0.21875
- up_weight: bfloat16 [768, 3072], replicated, may hold values from -0.21875 to 0.21875
- down_weight: bfloat16 [3072, 768], replicated, may hold values from -0.109375 to 0.109375
- head_weight: bfloat16 [768, 768], replicated, may hold values from -0.21875 to 0.21875
- head_gain: float32 [768], replicated, may hold values from 0.1 to 1.9
- vocab_weight: bfloat16 [16384, 768], P('term'), may hold values from -0.21875 to 0.21875
- vocab_bias: bfloat16 [16384], P('term'), may hold values from 0 to 2
- centroids: bfloat16 [16384, 768], P(('grp', 'term')), may hold values from -6 to 6
Outputs:
- sparse_weights: bfloat16 [128, 16384], P('grp', 'term')
- dense_slots: bfloat16 [32, 16, 768], P(('grp', 'term'))
- slot_passage: int32 [32, 16], P(('grp', 'term'))
The draws below stay inside these ranges and needn't reach their ends.
Inputs may be any that keep to these rules, and one draw needn't show every extreme that they name: `lengths`: the first token of every passage is live; some passage has all 128 tokens live. `block_list`: the live entries of a row are distinct term blocks and come first; the rest equal 128, which names no block. Every row has at least 48 live entries and at least one padding entry. The 4 passages of one device have distinct owners (cluster_ids // 512). No owner has more than 16 passages, and some owner has exactly 16.
All inputs are finite; a program needn't handle non-finite values.
Results may differ from the reference program's by a relative error of at most 0.007.
Values may be sent and summed in bfloat16 or wider, within the bound.
A program may use at most 128 MiB of HBM per device.

```python
import math
import jax
import jax.numpy as jnp
from jax import lax

D = 768
HEAD = 64
FF = 3072
VOCAB = 16384
BLOCK = 128
SEQ = 128
P_DEV = 4
NB = 96
CL_DEV = 512
CAP = 16
PASSAGES = 128
TOKENS = 16384
BLOCKS = 128
CLUSTERS = 16384
DEVICES = 32


def draw_hidden_states(key, part):
    values = jax.random.normal(key, (TOKENS, D), jnp.float32)
    return jnp.clip(values, -8.0, 8.0).astype(jnp.bfloat16)


def draw_attn_weight(key, part):
    values = jax.random.normal(key, (D, 3 * D), jnp.float32) / math.sqrt(D)
    return jnp.clip(values, -4.0, 4.0).astype(jnp.bfloat16)


def draw_lengths(key, part):
    drawn = jax.random.randint(key, (PASSAGES,), SEQ // 4, SEQ + 1)
    places = jnp.arange(PASSAGES, dtype=jnp.int32)
    drawn = jnp.where(places == 0, SEQ, drawn)
    drawn = jnp.where(places == 1, SEQ // 4, drawn)
    return drawn.astype(jnp.int32)


def draw_block_list(key, part):
    row_keys = jax.random.split(key, PASSAGES)
    chosen = jax.vmap(lambda row_key: jax.random.permutation(row_key, BLOCKS)[:NB])(row_keys)
    counts = jax.random.randint(jax.random.fold_in(key, 7), (PASSAGES, 1), NB // 2, NB)
    slots = jnp.arange(NB, dtype=jnp.int32)[None, :]
    return jnp.where(slots < counts, chosen, BLOCKS).astype(jnp.int32)


def draw_cluster_ids(key, part):
    mapping = jax.random.permutation(jax.random.fold_in(key, 31), DEVICES).astype(jnp.int32)
    offsets = jax.random.permutation(jax.random.fold_in(key, 32), DEVICES)[:P_DEV].astype(jnp.int32)
    senders = jnp.arange(DEVICES, dtype=jnp.int32)[:, None]
    owners = mapping[(senders + offsets[None, :]) % DEVICES]
    hottest = jax.random.randint(jax.random.fold_in(key, 33), (), 0, DEVICES).astype(jnp.int32)
    sends_hot = jnp.any(owners == hottest, axis=1)
    priority = jax.random.permutation(jax.random.fold_in(key, 34), DEVICES).astype(jnp.int32)
    score = jnp.where(sends_hot, DEVICES + priority, priority)
    order = jnp.argsort(score, stable=True)
    ranking = jnp.zeros((DEVICES,), jnp.int32).at[order].set(jnp.arange(DEVICES, dtype=jnp.int32))
    extra = ranking < 3 * P_DEV
    owners = owners.at[:, 0].set(jnp.where(extra, hottest, owners[:, 0]))
    within = jax.random.randint(jax.random.fold_in(key, 35), (DEVICES, P_DEV), 0, CL_DEV)
    return (owners * CL_DEV + within).reshape(PASSAGES).astype(jnp.int32)


def block_levels(stream_key, shape, pieces, low, high):
    loudness, own = 1.0, jax.random.fold_in(stream_key, 6)
    for position, parts in pieces:
        draws = jnp.exp(jax.random.uniform(jax.random.fold_in(own, position), (parts,), jnp.float32, low / len(pieces), high / len(pieces)))
        loudness = loudness * jnp.repeat(draws, shape[position] // parts).reshape([-1 if axis == position else 1 for axis in range(len(shape))])
    return loudness


def bell_draw(key, shape, deviation, reach, cuts=(), kind=jnp.bfloat16):
    entries = deviation * jax.random.normal(key, shape, jnp.float32)
    if cuts:
        entries = entries * block_levels(key, shape, cuts, -0.22, 0.18)
    return jnp.clip(entries, -reach, reach).astype(kind)


def setup_inputs(seed: int = 0) -> dict:
    key_of = jax.random.split(jax.random.key(seed), 14)
    hidden_states = draw_hidden_states(jax.random.fold_in(key_of[13], 71), 0)
    lengths = draw_lengths(jax.random.fold_in(key_of[13], 71), 0)
    block_list = draw_block_list(jax.random.fold_in(key_of[13], 71), 0)
    cluster_ids = draw_cluster_ids(jax.random.fold_in(key_of[13], 71), 0)
    attn_weight = draw_attn_weight(jax.random.fold_in(key_of[13], 71), 0)
    out_weight = bell_draw(key_of[5], (D, D), D ** -0.5, 0.21875)
    up_weight = bell_draw(key_of[6], (D, FF), D ** -0.5, 0.21875)
    down_weight = bell_draw(key_of[7], (FF, D), FF ** -0.5, 0.109375)
    head_weight = bell_draw(key_of[8], (D, D), D ** -0.5, 0.21875)
    head_gain = jnp.clip(1.0 + 0.18 * jax.random.normal(key_of[9], (D,), jnp.float32), 0.1, 1.9)
    vocab_weight = bell_draw(key_of[10], (VOCAB, D), D ** -0.5, 0.21875, ((0, 8),))
    vocab_bias = jnp.clip(2.0 * jax.random.uniform(key_of[11], (VOCAB,), jnp.float32) ** block_levels(key_of[11], (VOCAB,), ((0, 8),), -0.2, 0.2), 0.0, 2.0).astype(jnp.bfloat16)
    centroids = bell_draw(key_of[12], (CLUSTERS, D), 1.0, 6.0, ((0, 32),))
    return dict(hidden_states=hidden_states, lengths=lengths, block_list=block_list, cluster_ids=cluster_ids, attn_weight=attn_weight, out_weight=out_weight, up_weight=up_weight, down_weight=down_weight, head_weight=head_weight, head_gain=head_gain, vocab_weight=vocab_weight, vocab_bias=vocab_bias, centroids=centroids)


def layer_norm(values):
    center = values - lax.optimization_barrier(jnp.mean(values, axis=-1, keepdims=True))
    spread = lax.optimization_barrier(jnp.mean(center * center, axis=-1, keepdims=True))
    return center * lax.rsqrt(spread + 1e-06)

def encode(hidden_states, lengths, attn_weight, out_weight, up_weight, down_weight):
    passages = lengths.shape[0]
    seq_len = hidden_states.shape[0] // passages
    width = hidden_states.shape[1]
    head_count = width // HEAD
    joined = jnp.dot(hidden_states, attn_weight, preferred_element_type=jnp.float32).astype(jnp.bfloat16)
    joined = joined.reshape(passages, seq_len, 3, head_count, HEAD).astype(jnp.float32)
    query_heads = joined[:, :, 0]
    key_heads = joined[:, :, 1]
    value_heads = joined[:, :, 2]
    scores = jnp.einsum('pqhd,pkhd->phqk', query_heads, key_heads) / math.sqrt(HEAD)
    live_mask = jnp.arange(seq_len, dtype=jnp.int32)[None, :] < lengths[:, None]
    scores = jnp.where(live_mask[:, None, None, :], scores, -1e+30)
    highest = lax.optimization_barrier(jnp.max(scores, axis=-1, keepdims=True))
    expo = jnp.exp(scores - highest)
    attention = (expo / lax.optimization_barrier(jnp.sum(expo, axis=-1, keepdims=True))).astype(jnp.bfloat16)
    context = jnp.einsum('phqk,pkhd->pqhd', attention.astype(jnp.float32), value_heads)
    context = context.astype(jnp.bfloat16).reshape(passages * seq_len, width)
    mixed = hidden_states.astype(jnp.float32) + jnp.dot(context, out_weight, preferred_element_type=jnp.float32)
    first = layer_norm(mixed).astype(jnp.bfloat16)
    inner = jax.nn.gelu(jnp.dot(first, up_weight, preferred_element_type=jnp.float32), approximate=False).astype(jnp.bfloat16)
    second = first.astype(jnp.float32) + jnp.dot(inner, down_weight, preferred_element_type=jnp.float32)
    return layer_norm(second).astype(jnp.bfloat16)

def head_transform(layer_out, head_weight, head_gain):
    middle = jax.nn.gelu(jnp.dot(layer_out, head_weight, preferred_element_type=jnp.float32), approximate=False)
    return (layer_norm(middle) * head_gain[None, :]).astype(jnp.bfloat16)

def vocab_pool(transformed, lengths, block_list, vocab_weight, vocab_bias, first_col):
    logits = lax.dot_general(transformed, vocab_weight, (((1,), (1,)), ((), ())), preferred_element_type=jnp.float32)
    logits = logits + vocab_bias.astype(jnp.float32)[None, :]
    activity = jnp.log1p(jax.nn.relu(logits))
    passages = lengths.shape[0]
    seq_len = transformed.shape[0] // passages
    columns = vocab_weight.shape[0]
    activity = activity.reshape(passages, seq_len, columns)
    live_mask = (jnp.arange(seq_len, dtype=jnp.int32)[None, :] < lengths[:, None]).astype(jnp.float32)
    pooled = lax.optimization_barrier(jnp.max(activity * live_mask[:, :, None], axis=1))
    block_ids = (first_col + jnp.arange(columns, dtype=jnp.int32)) // BLOCK
    listed = jnp.any(block_list[:, :, None] == block_ids[None, None, :], axis=1)
    return jnp.where(listed, pooled, 0.0).astype(jnp.bfloat16)

def reference(hidden_states, lengths, block_list, cluster_ids, attn_weight, out_weight, up_weight, down_weight, head_weight, head_gain, vocab_weight, vocab_bias, centroids):

    def one_passage(inputs):
        tokens, length_one, listed_one = inputs
        layer_out = encode(tokens, length_one[None], attn_weight, out_weight, up_weight, down_weight)
        transformed = head_transform(layer_out, head_weight, head_gain)
        sparse_row = vocab_pool(transformed, length_one[None], listed_one[None, :], vocab_weight, vocab_bias, jnp.int32(0))
        return (sparse_row[0], layer_out[0])
    sparse_weights, dense_rows = lax.map(one_passage, (hidden_states.reshape(PASSAGES, SEQ, D), lengths, block_list))
    owner_ids = (cluster_ids // CL_DEV).astype(jnp.int32)
    residual = (dense_rows.astype(jnp.float32) - centroids[cluster_ids].astype(jnp.float32)).astype(jnp.bfloat16)
    places = jnp.arange(PASSAGES, dtype=jnp.int32)
    same_owner = owner_ids[:, None] == owner_ids[None, :]
    earlier = places[None, :] < places[:, None]
    ranks = lax.optimization_barrier(jnp.sum((same_owner & earlier).astype(jnp.int32), axis=1)).astype(jnp.int32)
    slot_index = (owner_ids * CAP + ranks).astype(jnp.int32)
    dense_flat = jnp.zeros((DEVICES * CAP, D), jnp.bfloat16).at[slot_index].set(residual)
    passage_flat = jnp.full((DEVICES * CAP,), -1, jnp.int32).at[slot_index].set(places)
    return (sparse_weights, dense_flat.reshape(DEVICES, CAP, D), passage_flat.reshape(DEVICES, CAP))
```

```python
import functools
import math

import jax
import jax.numpy as jnp
from jax import lax
from jax.experimental import pallas as pl
from jax.experimental.pallas import tpu as pltpu
from jax.sharding import PartitionSpec as P

HEAD = 64
BLOCK = 128
CL_DEV = 512
CAP = 16
MESH = pl.DeviceIdType.MESH
F32 = jnp.float32
BF16 = jnp.bfloat16


def norm(values):
    center = values - jnp.mean(values, axis=-1, keepdims=True)
    spread = jnp.mean(center * center, axis=-1, keepdims=True)
    return center * lax.rsqrt(spread + 1e-06)


def gelu(v):
    return (0.5 * v) * (1.0 + lax.erf(v * math.sqrt(0.5)))


def mm(a, b):
    return jnp.dot(a, b, preferred_element_type=F32)


def mm_nt(a, b):
    return lax.dot_general(a, b, (((1,), (1,)), ((), ())), preferred_element_type=F32)


def kernel(
    groups,
    n,
    side,
    seq,
    chunk_passages,
    len_ref,
    hid_ref,
    gain_ref,
    meta_ref,
    aw_hbm,
    ow_hbm,
    uw_hbm,
    dw_hbm,
    hw_hbm,
    voc_hbm,
    pool_out,
    dall_out,
    aw,
    ow,
    uw,
    dw,
    hw,
    voc,
    gath,
    joined,
    ctx,
    fst,
    inner,
    dacc,
    payload,
    dall,
    pool,
    rpool,
    wsem,
    tok_send,
    tok_recv,
    d_send,
    d_recv,
    x_send,
    x_recv,
):
    grp = lax.axis_index("grp")
    term = lax.axis_index("term")
    devices = groups * n
    me = grp * n + term
    chips = n // 2
    chip = term // 2
    core = term % 2
    partner = {"grp": grp, "term": chip * 2 + (1 - core)}
    cy, cx = chip // side, chip % side
    width = hid_ref.shape[1]
    rows = chunk_passages * seq
    chunks = hid_ref.shape[0] // rows
    ff = uw.shape[1]
    relay = side == 2
    half = rows // 2

    def other(k):
        ky, kx = k // side, k % side
        to = ((cy + ky) % side) * side + (cx + kx) % side
        return {"grp": grp, "term": to * 2 + core}

    def source(k):
        ky, kx = k // side, k % side
        return ((cy + side - ky) % side) * side + (cx + side - kx) % side

    def everyone(d):
        to = (me + d) % devices
        return {"grp": to // n, "term": to % n}

    loads = [
        pltpu.make_async_copy(src, dst, wsem.at[i])
        for i, (src, dst) in enumerate(
            [(aw_hbm, aw), (ow_hbm, ow), (uw_hbm, uw), (dw_hbm, dw), (hw_hbm, hw), (voc_hbm, voc.at[0])]
        )
    ]
    for load in loads:
        load.start()

    barrier = pltpu.get_barrier_semaphore()

    @pl.loop(1, devices)
    def _(d):
        pl.semaphore_signal(barrier, inc=1, device_id=everyone(d), device_id_type=MESH)

    def tok_copy(h, k):
        return pltpu.make_async_remote_copy(
            src_ref=gath.at[0, h],
            dst_ref=gath.at[k, h],
            send_sem=tok_send.at[h, k],
            recv_sem=tok_recv.at[h, k],
            device_id=other(k),
            device_id_type=MESH,
        )

    def relay_copy(h, part):
        via = 1 + part
        span = pl.ds(part * half, half)
        return pltpu.make_async_remote_copy(
            src_ref=gath.at[via, h, span],
            dst_ref=gath.at[3, h, span],
            send_sem=tok_send.at[h, 3 + part],
            recv_sem=tok_recv.at[h, 3 + part],
            device_id=other(2 - part),
            device_id_type=MESH,
        )

    voc_copy = pltpu.make_async_remote_copy(
        src_ref=voc_hbm,
        dst_ref=voc.at[1],
        send_sem=x_send.at[0],
        recv_sem=x_recv.at[0],
        device_id=partner,
        device_id_type=MESH,
    )
    pool_copy = pltpu.make_async_remote_copy(
        src_ref=pool.at[1],
        dst_ref=rpool,
        send_sem=x_send.at[1],
        recv_sem=x_recv.at[1],
        device_id=partner,
        device_id_type=MESH,
    )

    def dense_copy(d):
        return pltpu.make_async_remote_copy(
            src_ref=payload,
            dst_ref=dall.at[me],
            send_sem=d_send.at[d],
            recv_sem=d_recv.at[d],
            device_id=everyone(d),
            device_id_type=MESH,
        )

    def send_direct(h):
        if relay:
            tok_copy(h, 1).start()
            tok_copy(h, 2).start()
        else:

            @pl.loop(1, chips)
            def _(k):
                tok_copy(h, k).start()

    def send_relay(h):
        if relay:
            for part in range(2):
                tok_copy(h, 1 + part).wait_recv()
                relay_copy(h, part).start()

    def first_wait(h, i):
        @pl.when(h == 0)
        def _():
            loads[i].wait()

    dacc[...] = meta_ref[...]
    pairs = width // (2 * HEAD)
    lane = lax.broadcasted_iota(jnp.int32, (seq, 2 * HEAD), 1)
    key_place = lax.broadcasted_iota(jnp.int32, (2 * seq, seq), 1)
    row_place = lax.broadcasted_iota(jnp.int32, (seq, width), 0)
    low = lane < HEAD

    def encode(h, carry):
        x = hid_ref[pl.ds(pl.multiple_of(h * rows, rows), rows), :]
        first_wait(h, 0)
        for c in range(3):
            cols = slice(c * width, (c + 1) * width)
            joined[:, cols] = mm(x, aw[:, cols]).astype(BF16)

        def attend(p, carry):
            span = pl.ds(pl.multiple_of(p * seq, seq), seq)
            live = key_place < len_ref[h * chunk_passages + p]
            for pair in range(pairs):
                at = pair * 2 * HEAD
                q = joined[span, at : at + 2 * HEAD]
                k = joined[span, width + at : width + at + 2 * HEAD]
                v = joined[span, 2 * width + at : 2 * width + at + 2 * HEAD]
                zero = jnp.zeros_like(q)
                both = jnp.concatenate([jnp.where(low, q, zero), jnp.where(low, zero, q)], axis=0)
                scores = mm_nt(both, k) * (1.0 / math.sqrt(HEAD))
                scores = jnp.where(live, scores, -1e30)
                expo = jnp.exp(scores - jnp.max(scores, axis=-1, keepdims=True))
                att = (expo * (1.0 / jnp.sum(expo, axis=-1, keepdims=True))).astype(BF16)
                mixed = mm(att, v)
                ctx[span, at : at + 2 * HEAD] = jnp.where(low, mixed[:seq], mixed[seq:]).astype(BF16)
            return carry

        lax.fori_loop(0, chunk_passages, attend, 0)
        first_wait(h, 1)
        fst[...] = norm(x.astype(F32) + mm(ctx[...], ow[...])).astype(BF16)
        first_wait(h, 2)
        tile = 512

        def up(j, carry):
            cols = pl.ds(pl.multiple_of(j * tile, tile), tile)
            inner[:, cols] = gelu(mm(fst[...], uw[:, cols])).astype(BF16)
            return carry

        lax.fori_loop(0, ff // tile, up, 0)
        first_wait(h, 3)
        layer_out = norm(fst[...].astype(F32) + mm(inner[...], dw[...])).astype(BF16)
        wide = layer_out.astype(F32)
        for p in range(chunk_passages):
            dacc[pl.ds(h * chunk_passages + p, 1), :] = wide[p * seq : p * seq + 1]
        first_wait(h, 4)
        out = norm(gelu(mm(layer_out, hw[...]))) * gain_ref[...]
        for p in range(chunk_passages):
            one = out[p * seq : (p + 1) * seq]
            one = jnp.where(row_place < len_ref[h * chunk_passages + p], one, one[0:1])
            gath[0, h, p * seq : (p + 1) * seq, :] = one.astype(BF16)

        @pl.when(h == 0)
        def _():
            pl.semaphore_wait(barrier, devices - 1)
            voc_copy.start()

        @pl.when(h > 0)
        def _():
            send_relay(h - 1)

        @pl.when(h == chunks - 1)
        def _():
            payload[...] = dacc[...].astype(BF16)

        send_direct(h)

        @pl.when(h == chunks - 1)
        def _():
            @pl.loop(1, devices)
            def _(d):
                dense_copy(d).start()

        return carry

    lax.fori_loop(0, chunks, encode, 0)
    loads[5].wait()
    voc_copy.wait_recv()

    terms = voc_hbm.shape[0]
    tile = min(512, terms)
    per_part = terms // tile

    def score(h, k):
        c = source(k)

        def step(j, carry):
            part, at = j // per_part, pl.multiple_of((j % per_part) * tile, tile)
            logits = mm_nt(gath[k, h], voc[part, pl.ds(at, tile), :])
            for p in range(chunk_passages):
                best = jnp.max(logits[p * seq : (p + 1) * seq], axis=0, keepdims=True)
                pool[part, c, h * chunk_passages + p, :, pl.ds(at, tile)] = best
            return carry

        lax.fori_loop(0, 2 * per_part, step, 0)

    for h in range(chunks):
        score(h, 0)
    for h in range(chunks):
        if relay:
            if h == chunks - 1:
                send_relay(h)
            score(h, 1)
            score(h, 2)
            relay_copy(h, 0).wait_recv()
            relay_copy(h, 1).wait_recv()
            score(h, 3)
        else:

            @pl.loop(1, chips)
            def _(k):
                tok_copy(h, k).wait_recv()
                score(h, k)

    pool_copy.start()
    dall[me] = payload[...]

    @pl.loop(1, devices)
    def _(d):
        dense_copy(d).wait_recv()

    dall_out[...] = dall[...]

    @pl.loop(0, chips)
    def _(c):
        pool_out[c, core] = pool[0, c]

    pool_copy.wait_recv()

    @pl.loop(0, chips)
    def _(c):
        pool_out[c, 1 - core] = rpool[c]

    pool_copy.wait_send()
    voc_copy.wait_send()

    @pl.loop(1, devices)
    def _(d):
        dense_copy(d).wait_send()

    for h in range(chunks):
        if relay:
            tok_copy(h, 1).wait_send()
            tok_copy(h, 2).wait_send()
            relay_copy(h, 0).wait_send()
            relay_copy(h, 1).wait_send()
        else:

            @pl.loop(1, chips)
            def _(k):
                tok_copy(h, k).wait_send()


def place_rows(rows, passage_ids, clusters, valid, centroids, device_id):
    valid_int = valid.astype(jnp.int32)
    ranks = jnp.cumsum(valid_int) - 1
    selected = valid[None, :] & (ranks[None, :] == jnp.arange(CAP, dtype=jnp.int32)[:, None])
    picked = jnp.dot(selected.astype(BF16), rows, preferred_element_type=F32)
    selected_int = selected.astype(jnp.int32)
    filled = jnp.sum(selected_int, axis=1) > 0
    picked_passage = jnp.sum(selected_int * passage_ids[None, :], axis=1)
    local_ids = clusters - device_id * CL_DEV
    picked_local = jnp.sum(selected_int * local_ids[None, :], axis=1)
    lookup = (picked_local[:, None] == jnp.arange(CL_DEV, dtype=jnp.int32)[None, :]) & filled[
        :, None
    ]
    chosen = jnp.dot(lookup.astype(BF16), centroids, preferred_element_type=F32)
    residual = (picked - chosen).astype(BF16)
    dense_part = jnp.where(filled[:, None], residual, jnp.zeros((), BF16))
    slot_part = jnp.where(filled, picked_passage, -1).astype(jnp.int32)
    return (dense_part, slot_part)


def body(
    groups,
    n,
    hidden,
    lengths,
    block_list,
    cluster_ids,
    attn_weight,
    out_weight,
    up_weight,
    down_weight,
    head_weight,
    head_gain,
    vocab_weight,
    vocab_bias,
    centroids,
):
    passages = lengths.shape[0]
    tokens, width = hidden.shape
    seq = tokens // passages
    ff = up_weight.shape[1]
    terms = vocab_weight.shape[0]
    devices = groups * n
    chips = n // 2
    side = math.isqrt(chips)
    chunk_passages = 2
    chunks = passages // chunk_passages
    rows = chunk_passages * seq
    grp = lax.axis_index("grp")
    term = lax.axis_index("term")
    me = grp * n + term
    blocks = n * terms // BLOCK
    listed = jnp.any(
        block_list[:, :, None] == jnp.arange(blocks, dtype=jnp.int32)[None, None, :], axis=1
    )
    marks = jnp.concatenate(
        [
            listed.astype(F32),
            (cluster_ids // 256).astype(F32)[:, None],
            (cluster_ids % 256).astype(F32)[:, None],
            jnp.zeros((passages, width - blocks - 2), F32),
        ],
        axis=1,
    )
    meta = jnp.concatenate([jnp.zeros((passages, width), F32), marks], axis=0)
    vm = pl.BlockSpec(memory_space=pltpu.VMEM)
    hbm = pl.BlockSpec(memory_space=pl.ANY)
    dma = pltpu.SemaphoreType.DMA
    pool, dall = pl.pallas_call(
        functools.partial(kernel, groups, n, side, seq, chunk_passages),
        out_shape=(
            jax.ShapeDtypeStruct((chips, 2, passages, 1, terms), F32),
            jax.ShapeDtypeStruct((devices, 2 * passages, width), BF16),
        ),
        in_specs=[pl.BlockSpec(memory_space=pltpu.SMEM), vm, vm, vm] + [hbm] * 6,
        out_specs=(vm, vm),
        scratch_shapes=[
            pltpu.VMEM(attn_weight.shape, BF16),
            pltpu.VMEM(out_weight.shape, BF16),
            pltpu.VMEM(up_weight.shape, BF16),
            pltpu.VMEM(down_weight.shape, BF16),
            pltpu.VMEM(head_weight.shape, BF16),
            pltpu.VMEM((2, terms, width), BF16),
            pltpu.VMEM((chips, chunks, rows, width), BF16),
            pltpu.VMEM((rows, 3 * width), BF16),
            pltpu.VMEM((rows, width), BF16),
            pltpu.VMEM((rows, width), BF16),
            pltpu.VMEM((rows, ff), BF16),
            pltpu.VMEM((2 * passages, width), F32),
            pltpu.VMEM((2 * passages, width), BF16),
            pltpu.VMEM((devices, 2 * passages, width), BF16),
            pltpu.VMEM((2, chips, passages, 1, terms), F32),
            pltpu.VMEM((chips, passages, 1, terms), F32),
            dma((6,)),
            dma((chunks, chips + 1)),
            dma((chunks, chips + 1)),
            dma((devices,)),
            dma((devices,)),
            dma((2,)),
            dma((2,)),
        ],
        compiler_params=pltpu.CompilerParams(
            collective_id=0, has_side_effects=True, vmem_limit_bytes=60 * 1024 * 1024
        ),
    )(
        lengths,
        hidden,
        head_gain[None, :],
        meta,
        attn_weight,
        out_weight,
        up_weight,
        down_weight,
        head_weight,
        vocab_weight,
    )
    raw = pool.reshape(n * passages, terms)
    mine = lax.dynamic_slice_in_dim(dall, grp * n, n, 0)[:, passages:]
    flags = lax.dynamic_slice_in_dim(mine, term * (terms // BLOCK), terms // BLOCK, 2)
    flags = flags.reshape(n * passages, terms // BLOCK)
    value = jnp.log1p(jax.nn.relu(raw + vocab_bias.astype(F32)[None, :]))
    keep = jnp.repeat(flags, BLOCK, axis=1) > 0.5
    sparse = jnp.where(keep, value, 0.0).astype(BF16)
    ids = dall[:, passages:, blocks : blocks + 2].astype(jnp.int32)
    clusters = (ids[:, :, 0] * 256 + ids[:, :, 1]).reshape(devices * passages)
    dense_rows = dall[:, :passages].reshape(devices * passages, width)
    dense_part, slot_part = place_rows(
        dense_rows,
        jnp.arange(devices * passages, dtype=jnp.int32),
        clusters,
        clusters // CL_DEV == me,
        centroids,
        me,
    )
    return (sparse, dense_part[None, :, :], slot_part[None, :])


def solution(mesh):
    placed = (
        P(("grp", "term"), None),
        P(("grp", "term")),
        P(("grp", "term"), None),
        P(("grp", "term")),
        P(),
        P(),
        P(),
        P(),
        P(),
        P(),
        P("term", None),
        P("term"),
        P(("grp", "term"), None),
    )
    return jax.shard_map(
        functools.partial(body, mesh.shape["grp"], mesh.shape["term"]),
        mesh=mesh,
        in_specs=placed,
        out_specs=(P("grp", "term"), P(("grp", "term"), None, None), P(("grp", "term"), None)),
        check_vma=False,
    )
```

```python
import functools
import math

import jax
import jax.numpy as jnp
from jax import lax
from jax.experimental import pallas as pl
from jax.experimental.pallas import tpu as pltpu
from jax.sharding import PartitionSpec as P

HEAD = 64
BLOCK = 128
CL_DEV = 512
CAP = 16
MESH = pl.DeviceIdType.MESH
F32 = jnp.float32
BF16 = jnp.bfloat16


def norm(values):
    center = values - jnp.mean(values, axis=-1, keepdims=True)
    spread = jnp.mean(center * center, axis=-1, keepdims=True)
    return center * lax.rsqrt(spread + 1e-06)


def gelu(v):
    return (0.5 * v) * (1.0 + lax.erf(v * math.sqrt(0.5)))


def mm(a, b):
    return jnp.dot(a, b, preferred_element_type=F32)


def mm_nt(a, b):
    return lax.dot_general(a, b, (((1,), (1,)), ((), ())), preferred_element_type=F32)


def kernel(
    groups,
    n,
    side,
    seq,
    chunk_passages,
    len_ref,
    cid_ref,
    hid_ref,
    gain_ref,
    blk_ref,
    bias_ref,
    aw_hbm,
    ow_hbm,
    uw_hbm,
    dw_hbm,
    hw_hbm,
    voc_hbm,
    cen_hbm,
    sparse_out,
    dense_out,
    slot_out,
    aw,
    ow,
    uw,
    dw,
    hw,
    cen,
    voc,
    gath,
    joined,
    ctx,
    fst,
    inner,
    dacc,
    payload,
    dall,
    pool,
    res,
    wsem,
    tok_send,
    tok_recv,
    d_send,
    d_recv,
    x_send,
    x_recv,
):
    grp = lax.axis_index("grp")
    term = lax.axis_index("term")
    devices = groups * n
    me = grp * n + term
    chips = n // 2
    chip = term // 2
    core = term % 2
    partner = {"grp": grp, "term": chip * 2 + (1 - core)}
    cy, cx = chip // side, chip % side
    width = hid_ref.shape[1]
    rows = chunk_passages * seq
    chunks = hid_ref.shape[0] // rows
    ff = uw.shape[1]
    relay = side == 2
    half = rows // 2

    def other(k):
        ky, kx = k // side, k % side
        to = ((cy + ky) % side) * side + (cx + kx) % side
        return {"grp": grp, "term": to * 2 + core}

    def source(k):
        ky, kx = k // side, k % side
        return ((cy + side - ky) % side) * side + (cx + side - kx) % side

    def everyone(d):
        to = (me + d) % devices
        return {"grp": to // n, "term": to % n}

    loads = [
        pltpu.make_async_copy(src, dst, wsem.at[i])
        for i, (src, dst) in enumerate(
            [(aw_hbm, aw), (ow_hbm, ow), (uw_hbm, uw), (dw_hbm, dw), (hw_hbm, hw), (voc_hbm, voc.at[0]), (cen_hbm, cen)]
        )
    ]
    for load in loads:
        load.start()

    barrier = pltpu.get_barrier_semaphore()

    @pl.loop(1, devices)
    def _(d):
        pl.semaphore_signal(barrier, inc=1, device_id=everyone(d), device_id_type=MESH)

    def tok_copy(h, k):
        return pltpu.make_async_remote_copy(
            src_ref=gath.at[0, h],
            dst_ref=gath.at[k, h],
            send_sem=tok_send.at[h, k],
            recv_sem=tok_recv.at[h, k],
            device_id=other(k),
            device_id_type=MESH,
        )

    def relay_copy(h, part):
        via = 1 + part
        span = pl.ds(part * half, half)
        return pltpu.make_async_remote_copy(
            src_ref=gath.at[via, h, span],
            dst_ref=gath.at[3, h, span],
            send_sem=tok_send.at[h, 3 + part],
            recv_sem=tok_recv.at[h, 3 + part],
            device_id=other(2 - part),
            device_id_type=MESH,
        )

    voc_copy = pltpu.make_async_remote_copy(
        src_ref=voc_hbm,
        dst_ref=voc.at[1],
        send_sem=x_send.at[0],
        recv_sem=x_recv.at[0],
        device_id=partner,
        device_id_type=MESH,
    )
    pool_copy = pltpu.make_async_remote_copy(
        src_ref=pool,
        dst_ref=res.at[core],
        send_sem=x_send.at[1],
        recv_sem=x_recv.at[1],
        device_id=partner,
        device_id_type=MESH,
    )

    def dense_copy(d):
        return pltpu.make_async_remote_copy(
            src_ref=payload,
            dst_ref=dall.at[me],
            send_sem=d_send.at[d],
            recv_sem=d_recv.at[d],
            device_id=everyone(d),
            device_id_type=MESH,
        )

    def send_direct(h):
        if relay:
            tok_copy(h, 1).start()
            tok_copy(h, 2).start()
        else:

            @pl.loop(1, chips)
            def _(k):
                tok_copy(h, k).start()

    def send_relay(h):
        if relay:
            for part in range(2):
                tok_copy(h, 1 + part).wait_recv()
                relay_copy(h, part).start()

    def first_wait(h, i):
        @pl.when(h == 0)
        def _():
            loads[i].wait()

    passages = len_ref.shape[0]
    listing = blk_ref.shape[1]
    blocks = n * voc_hbm.shape[0] // BLOCK
    dacc[...] = jnp.zeros_like(dacc)
    square = lax.broadcasted_iota(jnp.int32, (listing, listing), 0) == lax.broadcasted_iota(
        jnp.int32, (listing, listing), 1
    )
    block_lane = lax.broadcasted_iota(jnp.int32, (listing, blocks), 1).astype(F32)
    id_lane = lax.broadcasted_iota(jnp.int32, (1, 128), 1)
    for p in range(passages):
        line = blk_ref[p : p + 1, :].astype(F32)
        column = jnp.sum(jnp.where(square, line, 0.0), axis=1, keepdims=True)
        marks = jnp.max(jnp.where(column == block_lane, 1.0, 0.0), axis=0, keepdims=True)
        dacc[passages + p : passages + p + 1, 0:blocks] = marks
        cid = cid_ref[p]
        ids = jnp.where(id_lane == 0, cid // 256, jnp.where(id_lane == 1, cid % 256, 0))
        dacc[passages + p : passages + p + 1, blocks : blocks + 128] = ids.astype(F32)
    pairs = width // (2 * HEAD)
    lane = lax.broadcasted_iota(jnp.int32, (seq, 2 * HEAD), 1)
    key_place = lax.broadcasted_iota(jnp.int32, (2 * seq, seq), 1)
    row_place = lax.broadcasted_iota(jnp.int32, (seq, width), 0)
    low = lane < HEAD

    def encode(h, carry):
        x = hid_ref[pl.ds(pl.multiple_of(h * rows, rows), rows), :]
        first_wait(h, 0)
        for c in range(3):
            cols = slice(c * width, (c + 1) * width)
            joined[:, cols] = mm(x, aw[:, cols]).astype(BF16)

        def attend(p, carry):
            span = pl.ds(pl.multiple_of(p * seq, seq), seq)
            live = key_place < len_ref[h * chunk_passages + p]
            for pair in range(pairs):
                at = pair * 2 * HEAD
                q = joined[span, at : at + 2 * HEAD]
                k = joined[span, width + at : width + at + 2 * HEAD]
                v = joined[span, 2 * width + at : 2 * width + at + 2 * HEAD]
                zero = jnp.zeros_like(q)
                both = jnp.concatenate([jnp.where(low, q, zero), jnp.where(low, zero, q)], axis=0)
                scores = mm_nt(both, k) * (1.0 / math.sqrt(HEAD))
                scores = jnp.where(live, scores, -1e30)
                expo = jnp.exp(scores - jnp.max(scores, axis=-1, keepdims=True))
                att = (expo * (1.0 / jnp.sum(expo, axis=-1, keepdims=True))).astype(BF16)
                mixed = mm(att, v)
                ctx[span, at : at + 2 * HEAD] = jnp.where(low, mixed[:seq], mixed[seq:]).astype(BF16)
            return carry

        lax.fori_loop(0, chunk_passages, attend, 0)
        first_wait(h, 1)
        fst[...] = norm(x.astype(F32) + mm(ctx[...], ow[...])).astype(BF16)
        first_wait(h, 2)
        tile = 512

        def up(j, carry):
            cols = pl.ds(pl.multiple_of(j * tile, tile), tile)
            inner[:, cols] = gelu(mm(fst[...], uw[:, cols])).astype(BF16)
            return carry

        lax.fori_loop(0, ff // tile, up, 0)
        first_wait(h, 3)
        layer_out = norm(fst[...].astype(F32) + mm(inner[...], dw[...])).astype(BF16)
        wide = layer_out.astype(F32)
        for p in range(chunk_passages):
            dacc[pl.ds(h * chunk_passages + p, 1), :] = wide[p * seq : p * seq + 1]
        first_wait(h, 4)
        out = norm(gelu(mm(layer_out, hw[...]))) * gain_ref[...]
        for p in range(chunk_passages):
            one = out[p * seq : (p + 1) * seq]
            one = jnp.where(row_place < len_ref[h * chunk_passages + p], one, one[0:1])
            gath[0, h, p * seq : (p + 1) * seq, :] = one.astype(BF16)

        @pl.when(h == 0)
        def _():
            pl.semaphore_wait(barrier, devices - 1)
            voc_copy.start()

        @pl.when(h > 0)
        def _():
            send_relay(h - 1)

        @pl.when(h == chunks - 1)
        def _():
            payload[...] = dacc[...].astype(BF16)

        send_direct(h)

        @pl.when(h == chunks - 1)
        def _():
            @pl.loop(1, devices)
            def _(d):
                dense_copy(d).start()

        return carry

    lax.fori_loop(0, chunks, encode, 0)
    loads[5].wait()
    voc_copy.wait_recv()

    terms = voc_hbm.shape[0]
    tile = min(1024, terms)
    per_part = terms // tile

    def score(h, k):
        c = source(k)

        def step(j, carry):
            part, at = j // per_part, pl.multiple_of((j % per_part) * tile, tile)
            logits = mm_nt(gath[k, h], voc[part, pl.ds(at, tile), :])
            for p in range(chunk_passages):
                best = jnp.max(logits[p * seq : (p + 1) * seq], axis=0, keepdims=True)
                row = pl.ds(c * passages + h * chunk_passages + p, 1)

                @pl.when(part == 0)
                def _():
                    res[core, row, pl.ds(at, tile)] = best

                @pl.when(part == 1)
                def _():
                    pool[row, pl.ds(at, tile)] = best
            return carry

        lax.fori_loop(0, 2 * per_part, step, 0)

    for h in range(chunks):
        score(h, 0)
    for h in range(chunks):
        if relay:
            if h == chunks - 1:
                send_relay(h)
            score(h, 1)
            score(h, 2)
            relay_copy(h, 0).wait_recv()
            relay_copy(h, 1).wait_recv()
            score(h, 3)
        else:

            @pl.loop(1, chips)
            def _(k):
                tok_copy(h, k).wait_recv()
                score(h, k)

    pool_copy.start()
    dall[me] = payload[...]

    @pl.loop(1, devices)
    def _(d):
        dense_copy(d).wait_recv()

    loads[6].wait()
    span = 2 * passages
    total = devices * span
    flat = dall[...].astype(F32).reshape(total, width)
    facts = flat[:, blocks : blocks + 128].astype(BF16)
    pick = lax.broadcasted_iota(jnp.int32, (8, 128), 0) == lax.broadcasted_iota(
        jnp.int32, (8, 128), 1
    )
    pieces = pltpu.roll(mm_nt(jnp.where(pick, 1.0, 0.0).astype(BF16), facts), total - passages, 1)
    clusters = pieces[0:1] * 256.0 + pieces[1:2]
    place = lax.broadcasted_iota(jnp.int32, (1, total), 1).astype(F32)
    sender = jnp.floor(place / span)
    within = place - sender * span
    first = (me * CL_DEV).astype(F32)
    local = clusters - first
    own = (within < passages) & (local >= 0.0) & (local < CL_DEV)
    own = jnp.where(own, 1.0, 0.0)
    before = lax.broadcasted_iota(jnp.int32, (total, total), 0) < lax.broadcasted_iota(
        jnp.int32, (total, total), 1
    )
    ranks = mm(
        jnp.broadcast_to(own, (8, total)).astype(BF16), jnp.where(before, 1.0, 0.0).astype(BF16)
    )[0:1]
    slot = lax.broadcasted_iota(jnp.int32, (CAP, total), 0).astype(F32)
    chosen = jnp.where((slot == ranks) & (own > 0.5), 1.0, 0.0)
    filled = jnp.sum(chosen, axis=1, keepdims=True) > 0.5
    passage = sender * passages + within
    number = jnp.sum(chosen * (passage + 1.0), axis=1, keepdims=True) - 1.0
    local = jnp.where(own > 0.5, local, 0.0)
    entry = jnp.sum(chosen * local, axis=1, keepdims=True)
    picked = mm(chosen.astype(BF16), flat.astype(BF16))
    entries = lax.broadcasted_iota(jnp.int32, (CAP, CL_DEV), 1).astype(F32)
    lookup = jnp.where((entries == entry) & filled, 1.0, 0.0).astype(BF16)
    dense_out[0] = jnp.where(filled, picked - mm(lookup, cen[...]), 0.0).astype(BF16)
    eye = lax.broadcasted_iota(jnp.int32, (CAP, CAP), 0) == lax.broadcasted_iota(
        jnp.int32, (CAP, CAP), 1
    )
    slot_out[...] = jnp.sum(jnp.where(eye, number, 0.0), axis=0, keepdims=True).astype(jnp.int32)

    peers = dall[pl.ds(grp * n, n), :, 0:blocks].astype(F32)
    marks = jnp.concatenate([peers[t, passages:] for t in range(n)], axis=0).astype(BF16)
    base = term * (terms // BLOCK)
    offset = (lax.broadcasted_iota(jnp.int32, (blocks, terms), 0) - base) * BLOCK
    column = lax.broadcasted_iota(jnp.int32, (blocks, terms), 1)
    spread = jnp.where((column >= offset) & (column < offset + BLOCK), 1.0, 0.0).astype(BF16)
    keep = mm(marks, spread) > 0.5

    pool_copy.wait_recv()
    both = []
    for c in range(chips):
        both += [res[s, c * passages : (c + 1) * passages] for s in range(2)]
    raw = jnp.concatenate(both, axis=0) + bias_ref[...].astype(F32)
    sparse_out[...] = jnp.where(keep, jnp.log1p(jnp.maximum(raw, 0.0)), 0.0).astype(BF16)

    pool_copy.wait_send()
    voc_copy.wait_send()

    @pl.loop(1, devices)
    def _(d):
        dense_copy(d).wait_send()

    for h in range(chunks):
        if relay:
            tok_copy(h, 1).wait_send()
            tok_copy(h, 2).wait_send()
            relay_copy(h, 0).wait_send()
            relay_copy(h, 1).wait_send()
        else:

            @pl.loop(1, chips)
            def _(k):
                tok_copy(h, k).wait_send()


def body(
    groups,
    n,
    hidden,
    lengths,
    block_list,
    cluster_ids,
    attn_weight,
    out_weight,
    up_weight,
    down_weight,
    head_weight,
    head_gain,
    vocab_weight,
    vocab_bias,
    centroids,
):
    passages = lengths.shape[0]
    tokens, width = hidden.shape
    seq = tokens // passages
    ff = up_weight.shape[1]
    terms = vocab_weight.shape[0]
    devices = groups * n
    chips = n // 2
    side = math.isqrt(chips)
    chunk_passages = 2
    chunks = passages // chunk_passages
    rows = chunk_passages * seq
    vm = pl.BlockSpec(memory_space=pltpu.VMEM)
    hbm = pl.BlockSpec(memory_space=pl.ANY)
    dma = pltpu.SemaphoreType.DMA
    return pl.pallas_call(
        functools.partial(kernel, groups, n, side, seq, chunk_passages),
        out_shape=(
            jax.ShapeDtypeStruct((n * passages, terms), BF16),
            jax.ShapeDtypeStruct((1, CAP, width), BF16),
            jax.ShapeDtypeStruct((1, CAP), jnp.int32),
        ),
        in_specs=[pl.BlockSpec(memory_space=pltpu.SMEM)] * 2 + [vm] * 4 + [hbm] * 7,
        out_specs=(vm, vm, vm),
        scratch_shapes=[
            pltpu.VMEM(attn_weight.shape, BF16),
            pltpu.VMEM(out_weight.shape, BF16),
            pltpu.VMEM(up_weight.shape, BF16),
            pltpu.VMEM(down_weight.shape, BF16),
            pltpu.VMEM(head_weight.shape, BF16),
            pltpu.VMEM(centroids.shape, BF16),
            pltpu.VMEM((2, terms, width), BF16),
            pltpu.VMEM((chips, chunks, rows, width), BF16),
            pltpu.VMEM((rows, 3 * width), BF16),
            pltpu.VMEM((rows, width), BF16),
            pltpu.VMEM((rows, width), BF16),
            pltpu.VMEM((rows, ff), BF16),
            pltpu.VMEM((2 * passages, width), F32),
            pltpu.VMEM((2 * passages, width), BF16),
            pltpu.VMEM((devices, 2 * passages, width), BF16),
            pltpu.VMEM((chips * passages, terms), F32),
            pltpu.VMEM((2, chips * passages, terms), F32),
            dma((7,)),
            dma((chunks, chips + 1)),
            dma((chunks, chips + 1)),
            dma((devices,)),
            dma((devices,)),
            dma((2,)),
            dma((2,)),
        ],
        compiler_params=pltpu.CompilerParams(
            collective_id=0, has_side_effects=True, vmem_limit_bytes=60 * 1024 * 1024
        ),
    )(
        lengths,
        cluster_ids,
        hidden,
        head_gain[None, :],
        block_list,
        vocab_bias[None, :],
        attn_weight,
        out_weight,
        up_weight,
        down_weight,
        head_weight,
        vocab_weight,
        centroids,
    )


def solution(mesh):
    placed = (
        P(("grp", "term"), None),
        P(("grp", "term")),
        P(("grp", "term"), None),
        P(("grp", "term")),
        P(),
        P(),
        P(),
        P(),
        P(),
        P(),
        P("term", None),
        P("term"),
        P(("grp", "term"), None),
    )
    return jax.shard_map(
        functools.partial(body, mesh.shape["grp"], mesh.shape["term"]),
        mesh=mesh,
        in_specs=placed,
        out_specs=(P("grp", "term"), P(("grp", "term"), None, None), P(("grp", "term"), None)),
        check_vma=False,
    )
```

```python
import functools
import math

import jax
import jax.numpy as jnp
from jax import lax
from jax.experimental import pallas as pl
from jax.experimental.pallas import tpu as pltpu
from jax.sharding import PartitionSpec as P

HEAD = 64
BLOCK = 128
CL_DEV = 512
CAP = 16
MESH = pl.DeviceIdType.MESH
F32 = jnp.float32
BF16 = jnp.bfloat16


def norm(values):
    center = values - jnp.mean(values, axis=-1, keepdims=True)
    spread = jnp.mean(center * center, axis=-1, keepdims=True)
    return center * lax.rsqrt(spread + 1e-06)


def gelu(v):
    return (0.5 * v) * (1.0 + lax.erf(v * math.sqrt(0.5)))


def mm(a, b):
    return jnp.dot(a, b, preferred_element_type=F32)


def mm_nt(a, b):
    return lax.dot_general(a, b, (((1,), (1,)), ((), ())), preferred_element_type=F32)


def kernel(
    groups,
    n,
    side,
    seq,
    chunk_passages,
    len_ref,
    cid_ref,
    hid_ref,
    gain_ref,
    blk_ref,
    bias_ref,
    aw_hbm,
    ow_hbm,
    uw_hbm,
    dw_hbm,
    hw_hbm,
    voc_hbm,
    cen_hbm,
    sparse_out,
    dense_out,
    slot_out,
    aw,
    ow,
    uw,
    dw,
    hw,
    cen,
    voc,
    gath,
    joined,
    ctx,
    fst,
    inner,
    dacc,
    payload,
    dall,
    pool,
    res,
    wsem,
    tok_send,
    tok_recv,
    d_send,
    d_recv,
    x_send,
    x_recv,
):
    grp = lax.axis_index("grp")
    term = lax.axis_index("term")
    devices = groups * n
    me = grp * n + term
    chips = n // 2
    chip = term // 2
    core = term % 2
    partner = {"grp": grp, "term": chip * 2 + (1 - core)}
    cy, cx = chip // side, chip % side
    width = hid_ref.shape[1]
    rows = chunk_passages * seq
    chunks = hid_ref.shape[0] // rows
    ff = uw.shape[1]
    relay = side == 2
    half = rows // 2

    def other(k):
        ky, kx = k // side, k % side
        to = ((cy + ky) % side) * side + (cx + kx) % side
        return {"grp": grp, "term": to * 2 + core}

    def source(k):
        ky, kx = k // side, k % side
        return ((cy + side - ky) % side) * side + (cx + side - kx) % side

    def everyone(d):
        to = (me + d) % devices
        return {"grp": to // n, "term": to % n}

    loads = [
        pltpu.make_async_copy(src, dst, wsem.at[i])
        for i, (src, dst) in enumerate(
            [(aw_hbm, aw), (ow_hbm, ow), (uw_hbm, uw), (dw_hbm, dw), (hw_hbm, hw), (voc_hbm, voc.at[0]), (cen_hbm, cen)]
        )
    ]
    for load in loads:
        load.start()

    barrier = pltpu.get_barrier_semaphore()

    @pl.loop(1, devices)
    def _(d):
        pl.semaphore_signal(barrier, inc=1, device_id=everyone(d), device_id_type=MESH)

    def tok_copy(h, k):
        return pltpu.make_async_remote_copy(
            src_ref=gath.at[0, h],
            dst_ref=gath.at[k, h],
            send_sem=tok_send.at[h, k],
            recv_sem=tok_recv.at[h, k],
            device_id=other(k),
            device_id_type=MESH,
        )

    def relay_copy(h, part):
        via = 1 + part
        span = pl.ds(part * half, half)
        return pltpu.make_async_remote_copy(
            src_ref=gath.at[via, h, span],
            dst_ref=gath.at[3, h, span],
            send_sem=tok_send.at[h, 3 + part],
            recv_sem=tok_recv.at[h, 3 + part],
            device_id=other(2 - part),
            device_id_type=MESH,
        )

    voc_copy = pltpu.make_async_remote_copy(
        src_ref=voc_hbm,
        dst_ref=voc.at[1],
        send_sem=x_send.at[0],
        recv_sem=x_recv.at[0],
        device_id=partner,
        device_id_type=MESH,
    )
    pool_copy = pltpu.make_async_remote_copy(
        src_ref=pool,
        dst_ref=res.at[core],
        send_sem=x_send.at[1],
        recv_sem=x_recv.at[1],
        device_id=partner,
        device_id_type=MESH,
    )

    def dense_copy(d):
        return pltpu.make_async_remote_copy(
            src_ref=payload,
            dst_ref=dall.at[me],
            send_sem=d_send.at[d],
            recv_sem=d_recv.at[d],
            device_id=everyone(d),
            device_id_type=MESH,
        )

    def send_direct(h):
        if relay:
            tok_copy(h, 1).start()
            tok_copy(h, 2).start()
        else:

            @pl.loop(1, chips)
            def _(k):
                tok_copy(h, k).start()

    def send_relay(h):
        if relay:
            for part in range(2):
                tok_copy(h, 1 + part).wait_recv()
                relay_copy(h, part).start()

    def first_wait(h, i):
        @pl.when(h == 0)
        def _():
            loads[i].wait()

    passages = len_ref.shape[0]
    listing = blk_ref.shape[1]
    blocks = n * voc_hbm.shape[0] // BLOCK
    dacc[...] = jnp.zeros_like(dacc)
    square = lax.broadcasted_iota(jnp.int32, (listing, listing), 0) == lax.broadcasted_iota(
        jnp.int32, (listing, listing), 1
    )
    block_lane = lax.broadcasted_iota(jnp.int32, (listing, blocks), 1).astype(F32)
    id_lane = lax.broadcasted_iota(jnp.int32, (1, 128), 1)
    for p in range(passages):
        line = blk_ref[p : p + 1, :].astype(F32)
        column = jnp.sum(jnp.where(square, line, 0.0), axis=1, keepdims=True)
        marks = jnp.max(jnp.where(column == block_lane, 1.0, 0.0), axis=0, keepdims=True)
        dacc[passages + p : passages + p + 1, 0:blocks] = marks
        cid = cid_ref[p]
        ids = jnp.where(id_lane == 0, cid // 256, jnp.where(id_lane == 1, cid % 256, 0))
        dacc[passages + p : passages + p + 1, blocks : blocks + 128] = ids.astype(F32)
    pairs = width // (2 * HEAD)
    lane = lax.broadcasted_iota(jnp.int32, (seq, 2 * HEAD), 1)
    key_place = lax.broadcasted_iota(jnp.int32, (2 * seq, seq), 1)
    row_place = lax.broadcasted_iota(jnp.int32, (seq, width), 0)
    low = lane < HEAD

    def encode(h, carry):
        x = hid_ref[pl.ds(pl.multiple_of(h * rows, rows), rows), :]
        first_wait(h, 0)
        for c in range(3):
            cols = slice(c * width, (c + 1) * width)
            joined[:, cols] = mm(x, aw[:, cols]).astype(BF16)

        @pl.when(h == 0)
        def _():
            pl.semaphore_wait(barrier, devices - 1)
            voc_copy.start()

        def attend(p, carry):
            span = pl.ds(pl.multiple_of(p * seq, seq), seq)
            live = key_place < len_ref[h * chunk_passages + p]
            for pair in range(pairs):
                at = pair * 2 * HEAD
                q = joined[span, at : at + 2 * HEAD]
                k = joined[span, width + at : width + at + 2 * HEAD]
                v = joined[span, 2 * width + at : 2 * width + at + 2 * HEAD]
                zero = jnp.zeros_like(q)
                both = jnp.concatenate([jnp.where(low, q, zero), jnp.where(low, zero, q)], axis=0)
                scores = mm_nt(both, k) * (1.0 / math.sqrt(HEAD))
                scores = jnp.where(live, scores, -1e30)
                expo = jnp.exp(scores - jnp.max(scores, axis=-1, keepdims=True))
                att = (expo * (1.0 / jnp.sum(expo, axis=-1, keepdims=True))).astype(BF16)
                mixed = mm(att, v)
                ctx[span, at : at + 2 * HEAD] = jnp.where(low, mixed[:seq], mixed[seq:]).astype(BF16)
            return carry

        lax.fori_loop(0, chunk_passages, attend, 0)
        first_wait(h, 1)
        fst[...] = norm(x.astype(F32) + mm(ctx[...], ow[...])).astype(BF16)
        first_wait(h, 2)
        tile = 1536

        def up(j, carry):
            cols = pl.ds(pl.multiple_of(j * tile, tile), tile)
            inner[:, cols] = gelu(mm(fst[...], uw[:, cols])).astype(BF16)
            return carry

        lax.fori_loop(0, ff // tile, up, 0)
        first_wait(h, 3)
        layer_out = norm(fst[...].astype(F32) + mm(inner[...], dw[...])).astype(BF16)
        wide = layer_out.astype(F32)
        for p in range(chunk_passages):
            dacc[pl.ds(h * chunk_passages + p, 1), :] = wide[p * seq : p * seq + 1]
        first_wait(h, 4)
        out = norm(gelu(mm(layer_out, hw[...]))) * gain_ref[...][None, :]
        for p in range(chunk_passages):
            one = out[p * seq : (p + 1) * seq]
            one = jnp.where(row_place < len_ref[h * chunk_passages + p], one, one[0:1])
            gath[0, h, p * seq : (p + 1) * seq, :] = one.astype(BF16)

        @pl.when(h > 0)
        def _():
            send_relay(h - 1)

        @pl.when(h == chunks - 1)
        def _():
            payload[...] = dacc[...].astype(BF16)

        send_direct(h)

        @pl.when(h == chunks - 1)
        def _():
            @pl.loop(1, devices)
            def _(d):
                dense_copy(d).start()

        return carry

    lax.fori_loop(0, chunks, encode, 0)
    terms = voc_hbm.shape[0]
    tile = min(2048, terms)
    per_part = terms // tile

    def score(h, k, parts=(1, 0)):
        c = source(k)
        for part in parts:
            for j in range(per_part):
                cols = slice(j * tile, (j + 1) * tile)
                logits = mm_nt(gath[k, h], voc[part, cols, :])
                for p in range(chunk_passages):
                    best = jnp.max(logits[p * seq : (p + 1) * seq], axis=0, keepdims=True)
                    row = pl.ds(c * passages + h * chunk_passages + p, 1)
                    if part == 0:
                        res[core, row, cols] = best
                    else:
                        pool[row, cols] = best

    loads[5].wait()

    @pl.loop(0, chunks)
    def _(h):
        score(h, 0, (0,))

    voc_copy.wait_recv()

    @pl.loop(0, chunks)
    def _(h):
        score(h, 0, (1,))

    if relay:
        last = chunks - 1

        @pl.loop(0, 2 * chunks)
        def _(i):
            @pl.when(i == 2 * last)
            def _():
                send_relay(last)

            score(i // 2, 1 + i % 2)

        @pl.loop(0, chunks)
        def _(h):
            relay_copy(h, 0).wait_recv()
            relay_copy(h, 1).wait_recv()
            score(h, 3, (1,))

        pool_copy.start()

        @pl.loop(0, chunks)
        def _(h):
            score(h, 3, (0,))
    else:

        @pl.loop(0, chunks)
        def _(h):
            @pl.loop(1, chips)
            def _(k):
                tok_copy(h, k).wait_recv()
                score(h, k)

        pool_copy.start()

    dall[me] = payload[...]

    @pl.loop(1, devices)
    def _(d):
        dense_copy(d).wait_recv()

    loads[6].wait()
    span = 2 * passages
    total = devices * span
    flat = dall[...].astype(F32).reshape(total, width)
    facts = flat[:, blocks : blocks + 128].astype(BF16)
    pick = lax.broadcasted_iota(jnp.int32, (8, 128), 0) == lax.broadcasted_iota(
        jnp.int32, (8, 128), 1
    )
    pieces = pltpu.roll(mm_nt(jnp.where(pick, 1.0, 0.0).astype(BF16), facts), total - passages, 1)
    clusters = pieces[0:1] * 256.0 + pieces[1:2]
    place = lax.broadcasted_iota(jnp.int32, (1, total), 1).astype(F32)
    sender = jnp.floor(place / span)
    within = place - sender * span
    first = (me * CL_DEV).astype(F32)
    local = clusters - first
    own = (within < passages) & (local >= 0.0) & (local < CL_DEV)
    own = jnp.where(own, 1.0, 0.0)
    before = lax.broadcasted_iota(jnp.int32, (total, total), 0) < lax.broadcasted_iota(
        jnp.int32, (total, total), 1
    )
    ranks = mm(
        jnp.broadcast_to(own, (8, total)).astype(BF16), jnp.where(before, 1.0, 0.0).astype(BF16)
    )[0:1]
    slot = lax.broadcasted_iota(jnp.int32, (CAP, total), 0).astype(F32)
    chosen = jnp.where((slot == ranks) & (own > 0.5), 1.0, 0.0)
    filled = jnp.sum(chosen, axis=1, keepdims=True) > 0.5
    passage = sender * passages + within
    number = jnp.sum(chosen * (passage + 1.0), axis=1, keepdims=True) - 1.0
    local = jnp.where(own > 0.5, local, 0.0)
    entry = jnp.sum(chosen * local, axis=1, keepdims=True)
    picked = mm(chosen.astype(BF16), flat.astype(BF16))
    entries = lax.broadcasted_iota(jnp.int32, (CAP, CL_DEV), 1).astype(F32)
    lookup = jnp.where((entries == entry) & filled, 1.0, 0.0).astype(BF16)
    dense_out[0] = jnp.where(filled, picked - mm(lookup, cen[...]), 0.0).astype(BF16)
    eye = lax.broadcasted_iota(jnp.int32, (CAP, CAP), 0) == lax.broadcasted_iota(
        jnp.int32, (CAP, CAP), 1
    )
    slot_out[...] = jnp.sum(jnp.where(eye, number, 0.0), axis=0, keepdims=True).astype(jnp.int32)

    peers = dall[pl.ds(grp * n, n), :, 0:blocks].astype(F32)
    marks = jnp.concatenate([peers[t, passages:] for t in range(n)], axis=0).astype(BF16)
    base = term * (terms // BLOCK)
    offset = (lax.broadcasted_iota(jnp.int32, (blocks, terms), 0) - base) * BLOCK
    column = lax.broadcasted_iota(jnp.int32, (blocks, terms), 1)
    spread = jnp.where((column >= offset) & (column < offset + BLOCK), 1.0, 0.0).astype(BF16)
    keep = mm(marks, spread) > 0.5

    pool_copy.wait_recv()
    both = []
    for c in range(chips):
        both += [res[s, c * passages : (c + 1) * passages] for s in range(2)]
    raw = jnp.concatenate(both, axis=0) + bias_ref[...].astype(F32)[None, :]
    sparse_out[...] = jnp.where(keep, jnp.log1p(jnp.maximum(raw, 0.0)), 0.0).astype(BF16)

    pool_copy.wait_send()
    voc_copy.wait_send()

    @pl.loop(1, devices)
    def _(d):
        dense_copy(d).wait_send()

    for h in range(chunks):
        if relay:
            tok_copy(h, 1).wait_send()
            tok_copy(h, 2).wait_send()
            relay_copy(h, 0).wait_send()
            relay_copy(h, 1).wait_send()
        else:

            @pl.loop(1, chips)
            def _(k):
                tok_copy(h, k).wait_send()


def body(
    groups,
    n,
    hidden,
    lengths,
    block_list,
    cluster_ids,
    attn_weight,
    out_weight,
    up_weight,
    down_weight,
    head_weight,
    head_gain,
    vocab_weight,
    vocab_bias,
    centroids,
):
    passages = lengths.shape[0]
    tokens, width = hidden.shape
    seq = tokens // passages
    ff = up_weight.shape[1]
    terms = vocab_weight.shape[0]
    devices = groups * n
    chips = n // 2
    side = math.isqrt(chips)
    chunk_passages = 2
    chunks = passages // chunk_passages
    rows = chunk_passages * seq
    vm = pl.BlockSpec(memory_space=pltpu.VMEM)
    hbm = pl.BlockSpec(memory_space=pl.ANY)
    dma = pltpu.SemaphoreType.DMA
    return pl.pallas_call(
        functools.partial(kernel, groups, n, side, seq, chunk_passages),
        out_shape=(
            jax.ShapeDtypeStruct((n * passages, terms), BF16),
            jax.ShapeDtypeStruct((1, CAP, width), BF16),
            jax.ShapeDtypeStruct((1, CAP), jnp.int32),
        ),
        in_specs=[pl.BlockSpec(memory_space=pltpu.SMEM)] * 2 + [vm] * 4 + [hbm] * 7,
        out_specs=(vm, vm, vm),
        scratch_shapes=[
            pltpu.VMEM(attn_weight.shape, BF16),
            pltpu.VMEM(out_weight.shape, BF16),
            pltpu.VMEM(up_weight.shape, BF16),
            pltpu.VMEM(down_weight.shape, BF16),
            pltpu.VMEM(head_weight.shape, BF16),
            pltpu.VMEM(centroids.shape, BF16),
            pltpu.VMEM((2, terms, width), BF16),
            pltpu.VMEM((chips, chunks, rows, width), BF16),
            pltpu.VMEM((rows, 3 * width), BF16),
            pltpu.VMEM((rows, width), BF16),
            pltpu.VMEM((rows, width), BF16),
            pltpu.VMEM((rows, ff), BF16),
            pltpu.VMEM((2 * passages, width), F32),
            pltpu.VMEM((2 * passages, width), BF16),
            pltpu.VMEM((devices, 2 * passages, width), BF16),
            pltpu.VMEM((chips * passages, terms), F32),
            pltpu.VMEM((2, chips * passages, terms), F32),
            dma((7,)),
            dma((chunks, chips + 1)),
            dma((chunks, chips + 1)),
            dma((devices,)),
            dma((devices,)),
            dma((2,)),
            dma((2,)),
        ],
        compiler_params=pltpu.CompilerParams(
            collective_id=0, has_side_effects=True, vmem_limit_bytes=60 * 1024 * 1024
        ),
    )(
        lengths,
        cluster_ids,
        hidden,
        head_gain,
        block_list,
        vocab_bias,
        attn_weight,
        out_weight,
        up_weight,
        down_weight,
        head_weight,
        vocab_weight,
        centroids,
    )


def solution(mesh):
    placed = (
        P(("grp", "term"), None),
        P(("grp", "term")),
        P(("grp", "term"), None),
        P(("grp", "term")),
        P(),
        P(),
        P(),
        P(),
        P(),
        P(),
        P("term", None),
        P("term"),
        P(("grp", "term"), None),
    )
    return jax.shard_map(
        functools.partial(body, mesh.shape["grp"], mesh.shape["term"]),
        mesh=mesh,
        in_specs=placed,
        out_specs=(P("grp", "term"), P(("grp", "term"), None, None), P(("grp", "term"), None)),
        check_vma=False,
    )
```
